512 devices in a mesh: traj: 4 (over x), slab: 128 (over z, y, core).
Axes of the slice: x: 4, y: 8, z: 8, core: 2. Of those that a mesh axis runs over, the one named last changes fastest.
Arguments:
- grad_out: bfloat16 [1024, 384, 128], P(('traj', 'slab')), parts along dimension 0, may hold values from -96 to 96
- cached: bfloat16 [1024, 384, 128], P('traj', 'slab'), parts along dimension 0, may hold values from -0.059814453 to 0.059814453
- values: bfloat16 [1024, 384, 128], P(('traj', 'slab')), parts along dimension 0, may hold values from -0.75 to 0.75
- query_x: bfloat16 [1024, 128], P('traj'), parts along dimension 0, may hold values from -6 to 6
- key_x: bfloat16 [1024, 128], P('traj'), parts along dimension 0, may hold values from -6 to 6
- query_y: bfloat16 [1536, 128], P('traj'), parts along dimension 0, may hold values from -6 to 6
- key_y: bfloat16 [1536, 128], P('traj'), parts along dimension 0, may hold values from -6 to 6
Outputs:
- grad_values: bfloat16 [1024, 384, 128], P(('traj', 'slab')), parts along dimension 0
- query_x_grad: float32 [1024, 128], P(('traj', 'slab')), parts along dimension 0
- key_x_grad: float32 [1024, 128], P(('traj', 'slab')), parts along dimension 0
- query_y_grad: float32 [1536, 128], P(('traj', 'slab')), parts along dimension 0
- key_y_grad: float32 [1536, 128], P(('traj', 'slab')), parts along dimension 0
The draws below stay inside these ranges and needn't reach their ends.
There are 4 independent parts, one for each index of `traj`. The reference program is written for one: setup_inputs(seed, part) draws one part's arguments, and reference() takes and returns one part's arrays. A program takes and returns all parts, laid end to end along the dimension named above; each array names one. Nothing has to cross between parts.
All inputs are finite; a program needn't handle non-finite values.
Results may differ from the reference program's by a relative error of at most 0.0067.
Values may be sent and summed in bfloat16 or wider, within the bound.
No kernel may reach another device: no remote copies, remote signals or barrier semaphores. Data moves between devices by JAX's collectives and lax.ppermute only.
A program may use at most 64 MiB of HBM per device.

```python
import math
import jax
import jax.numpy as jnp
from jax import lax

HEADS = 4
HEAD = 32
CHANNELS = 128
NX = 256
NY = 384


def factor_pair(key, length):
    pieces = jax.random.split(key, 2)
    queries = jnp.clip(1.4 * jax.random.normal(pieces[0], (length, CHANNELS), jnp.float32), -6.0, 6.0)
    key_rows = jnp.clip(1.4 * jax.random.normal(pieces[1], (length, CHANNELS), jnp.float32), -6.0, 6.0)
    return (queries, key_rows)


def draw_query_x(key, part):
    return factor_pair(jax.random.fold_in(key, 11), NX)[0].astype(jnp.bfloat16)


def draw_key_x(key, part):
    return factor_pair(jax.random.fold_in(key, 11), NX)[1].astype(jnp.bfloat16)


def draw_query_y(key, part):
    return factor_pair(jax.random.fold_in(key, 12), NY)[0].astype(jnp.bfloat16)


def draw_key_y(key, part):
    return factor_pair(jax.random.fold_in(key, 12), NY)[1].astype(jnp.bfloat16)


def with_spikes(array, rng, source, target, shards_of, factor):
    def block_of(dim):
        return (jnp.arange(array.shape[dim]) // (array.shape[dim] // shards_of)).reshape((-1,) + (1,) * (array.ndim - 1 - dim))

    first = jax.random.permutation(rng, shards_of)[block_of(target)]
    far = (block_of(target) + shards_of // 2) % shards_of
    return jnp.where((block_of(source) == first) | (block_of(source) == far), factor * array, array)


def levels(stream_key, shape, shards, low, high):
    level = 1.0
    for dim, shards_of in shards:
        heights = jax.random.uniform(jax.random.fold_in(jax.random.fold_in(stream_key, 6), dim), (shards_of,), jnp.float32, low / len(shards), high / len(shards))
        level = level * jnp.repeat(jnp.exp(heights), shape[dim] // shards_of).reshape((-1,) + (1,) * (len(shape) - 1 - dim))
    return level


def noise(stream_key, shape, spread, reach, shards=(), dtype=jnp.bfloat16):
    array = spread * jax.random.normal(stream_key, shape, jnp.float32)
    if shards:
        array = array * levels(stream_key, shape, shards, -0.22, 0.18)
    return jnp.clip(array, -reach, reach).astype(dtype)


def heavy_noise(stream_key, dims, spread, most, shards, heavy, dtype=jnp.bfloat16):
    values = spread * jax.random.normal(stream_key, dims, jnp.float32)
    if shards:
        values = values * levels(stream_key, dims, shards, -0.22, 0.18)
    return jnp.clip(with_spikes(values, jax.random.fold_in(stream_key, 3), *heavy), -most, most).astype(dtype)


def setup_inputs(seed: int = 0, part: int = 0) -> dict:
    arg_keys = jax.random.split(jax.random.key(seed), 8)
    part_keys = jax.random.split(jax.random.fold_in(arg_keys[7], part), 8)
    return {
        "grad_out": heavy_noise(part_keys[0], (NX, NY, CHANNELS), 4.0, 96.0, ((0, 128),), (1, 0, 128, 5.5)),
        "cached": noise(part_keys[1], (NX, NY, CHANNELS), 0.01, 0.059814453, ((1, 128),)),
        "values": heavy_noise(part_keys[2], (NX, NY, CHANNELS), 0.03, 0.75, ((0, 128),), (0, 1, 128, 5.5)),
        "query_x": draw_query_x(jax.random.fold_in(jax.random.fold_in(arg_keys[7], part), 71), part),
        "key_x": draw_key_x(jax.random.fold_in(jax.random.fold_in(arg_keys[7], part), 71), part),
        "query_y": draw_query_y(jax.random.fold_in(jax.random.fold_in(arg_keys[7], part), 71), part),
        "key_y": draw_key_y(jax.random.fold_in(jax.random.fold_in(arg_keys[7], part), 71), part),
    }


def axis_kernel(queries, key_rows):
    scores = jnp.dot(queries, key_rows.T, preferred_element_type=jnp.float32) / math.sqrt(HEAD)
    return jax.nn.softmax(scores, axis=1)

def factor_grads(kernel, coupling, queries, key_rows):
    row_delta = lax.optimization_barrier(jnp.sum(kernel * coupling, axis=1))
    weighted = kernel * (coupling - row_delta[:, None])
    grad_query = jnp.dot(weighted, key_rows.astype(jnp.float32), precision=lax.Precision.HIGHEST) / math.sqrt(HEAD)
    grad_key = jnp.dot(weighted.T, queries.astype(jnp.float32), precision=lax.Precision.HIGHEST) / math.sqrt(HEAD)
    return (grad_query, grad_key)

def reference(grad_out, cached, values, query_x, key_x, query_y, key_y):
    mixed_heads = []
    qx_terms = []
    kx_terms = []
    for head_index in range(HEADS):
        offset = head_index * HEAD
        head_query = query_x[:, offset:offset + HEAD]
        head_key = key_x[:, offset:offset + HEAD]
        kernel = axis_kernel(head_query, head_key)
        grad_rows = grad_out[:, :, offset:offset + HEAD].reshape(NX, NY * HEAD)
        saved_rows = cached[:, :, offset:offset + HEAD].reshape(NX, NY * HEAD)
        grad_mixed = lax.dot_general(kernel.astype(jnp.bfloat16), grad_rows, (((0,), (0,)), ((), ())), preferred_element_type=jnp.float32).astype(jnp.bfloat16)
        coupling = lax.dot_general(grad_rows, saved_rows, (((1,), (1,)), ((), ())), preferred_element_type=jnp.float32)
        grad_query, grad_key = factor_grads(kernel, coupling, head_query, head_key)
        qx_terms.append(grad_query)
        kx_terms.append(grad_key)
        mixed_heads.append(grad_mixed.reshape(NX, NY, HEAD))
    value_heads = []
    qy_terms = []
    ky_terms = []
    for head_index in range(HEADS):
        offset = head_index * HEAD
        head_query = query_y[:, offset:offset + HEAD]
        head_key = key_y[:, offset:offset + HEAD]
        kernel = axis_kernel(head_query, head_key)
        kernel_low = lax.optimization_barrier(kernel.astype(jnp.bfloat16)).astype(jnp.float32)
        mixed_head = mixed_heads[head_index].astype(jnp.float32)
        value_head = values[:, :, offset:offset + HEAD].astype(jnp.float32)
        grad_value = jnp.einsum('jk,xje->xke', kernel_low, mixed_head, precision=lax.Precision.HIGHEST)
        coupling = jnp.einsum('xje,xke->jk', mixed_head, value_head, precision=lax.Precision.HIGHEST)
        grad_query, grad_key = factor_grads(kernel, coupling, head_query, head_key)
        qy_terms.append(grad_query)
        ky_terms.append(grad_key)
        value_heads.append(grad_value.astype(jnp.bfloat16))
    return (jnp.concatenate(value_heads, axis=2), jnp.concatenate(qx_terms, axis=1), jnp.concatenate(kx_terms, axis=1), jnp.concatenate(qy_terms, axis=1), jnp.concatenate(ky_terms, axis=1))
```

```python
import functools
import math

import jax
import jax.numpy as jnp
from jax import lax
from jax.experimental import pallas as pl
from jax.experimental.pallas import tpu as pltpu
from jax.sharding import PartitionSpec as P

HEAD = 32
LANES = 128
XR = 2
YU = 3
TILES = XR * YU
SEND = 3 * TILES
BACK = TILES + 4
F32 = jnp.float32
BF16 = jnp.bfloat16
ROOT = math.sqrt(HEAD)


def dot(a, b, dims=((1,), (0,))):
    return lax.dot_general(a, b, (dims, ((), ())), preferred_element_type=F32)


def pack_kernel(grad_ref, cached_ref, values_ref, out_ref, rows_ref, send_ref):
    for part, ref in enumerate((grad_ref, cached_ref, values_ref)):
        rows_ref[...] = ref[...].reshape(TILES * LANES, LANES).astype(F32)
        for u in range(YU):
            for r in range(XR):
                if part == 1:
                    tile = rows_ref[pl.ds(u * XR * LANES + r, LANES, stride=XR), :]
                else:
                    tile = rows_ref[pl.ds(r * YU * LANES + u, LANES, stride=YU), :]
                send_ref[pl.ds(part * TILES + u * XR + r, LANES, stride=SEND), :] = tile.T
    out_ref[...] = send_ref[...].astype(BF16)


def softmax_kernel(
    query_x_ref, key_x_ref, query_y_ref, key_y_ref,
    kernel_x_ref, kernel_xt_ref, kernel_y_ref, low_y_ref,
    tiled_qx_ref, tiled_kx_ref, tiled_qy_ref, tiled_ky_ref,
    rows_ref,
):
    head = lax.axis_index("slab") // HEAD
    source = lax.broadcasted_iota(jnp.int32, (LANES, LANES), 0)
    lane = lax.broadcasted_iota(jnp.int32, (LANES, LANES), 1)
    spread = (source == head * HEAD + lane % HEAD).astype(BF16)

    def permuted(ref, step):
        rows_ref[0 : step * LANES, :] = ref[...].astype(F32)
        return jnp.concatenate(
            [rows_ref[pl.ds(r, LANES, stride=step), :] for r in range(step)], axis=0
        ).astype(BF16)

    def softmax(tiled_q, tiled_k):
        first = lax.broadcasted_iota(jnp.int32, tiled_q.shape, 1) < HEAD
        scores = dot(jnp.where(first, tiled_q, 0), tiled_k, ((1,), (1,))) / ROOT
        top = jnp.max(scores, axis=1, keepdims=True)
        power = jnp.exp(scores - top)
        return power / jnp.sum(power, axis=1, keepdims=True)

    tiled_qx = dot(permuted(query_x_ref, XR), spread).astype(BF16)
    tiled_kx = dot(permuted(key_x_ref, XR), spread).astype(BF16)
    tiled_qy = dot(permuted(query_y_ref, YU), spread).astype(BF16)
    tiled_ky = dot(permuted(key_y_ref, YU), spread).astype(BF16)
    kernel_x = softmax(tiled_qx, tiled_kx)
    kernel_y = softmax(tiled_qy, tiled_ky)
    kernel_x_ref[...] = kernel_x
    kernel_xt_ref[...] = kernel_x.T.astype(BF16)
    kernel_y_ref[...] = kernel_y
    low_y_ref[...] = kernel_y.astype(BF16)
    tiled_qx_ref[...] = tiled_qx
    tiled_kx_ref[...] = tiled_kx
    tiled_qy_ref[...] = tiled_qy
    tiled_ky_ref[...] = tiled_ky


def channel_kernel(
    field_ref,
    kernel_x_ref, kernel_xt_ref, kernel_y_ref, low_y_ref,
    tiled_qx_ref, tiled_kx_ref, tiled_qy_ref, tiled_ky_ref,
    out_ref, rows_ref, back_ref,
):
    rows_ref[...] = field_ref[...].astype(F32)

    def tile(q):
        return rows_ref[pl.ds(q, LANES, stride=SEND), :].astype(BF16)

    def field(part):
        return jnp.concatenate(
            [
                jnp.concatenate([tile(part * TILES + u * XR + r) for u in range(YU)], axis=1)
                for r in range(XR)
            ],
            axis=0,
        )

    grad = field(0)
    values = field(2)
    cached = jnp.concatenate(
        [
            jnp.concatenate([tile(TILES + u * XR + r) for r in range(XR)], axis=1)
            for u in range(YU)
        ],
        axis=0,
    )
    mixed = dot(kernel_xt_ref[...], grad).astype(BF16)
    grad_values = dot(mixed, low_y_ref[...])
    for u in range(YU):
        for r in range(XR):
            back_ref[pl.ds(u * XR + r, LANES, stride=BACK), :] = grad_values[
                r * LANES : (r + 1) * LANES, u * LANES : (u + 1) * LANES
            ]

    def factor_grads(kernel, coupling, tiled_q, tiled_k):
        delta = jnp.sum(kernel * coupling, axis=1, keepdims=True)
        weighted = kernel * (coupling - delta) / ROOT
        high = weighted.astype(BF16)
        low = (weighted - high.astype(F32)).astype(BF16)
        grad_query = dot(high, tiled_k) + dot(low, tiled_k)
        grad_key = dot(high, tiled_q, ((0,), (0,))) + dot(low, tiled_q, ((0,), (0,)))
        return grad_query, grad_key

    query_x, key_x = factor_grads(
        kernel_x_ref[...], dot(grad, cached), tiled_qx_ref[...], tiled_kx_ref[...]
    )
    query_y, key_y = factor_grads(
        kernel_y_ref[...], dot(mixed, values, ((0,), (0,))), tiled_qy_ref[...], tiled_ky_ref[...]
    )
    slots = [query_x[r * LANES : (r + 1) * LANES] for r in range(XR)]
    slots += [key_x[r * LANES : (r + 1) * LANES] for r in range(XR)]
    slots += [query_y[u * LANES : (u + 1) * LANES] for u in range(YU)]
    slots += [key_y[u * LANES : (u + 1) * LANES] for u in range(YU)]
    group = lax.broadcasted_iota(jnp.int32, (LANES, LANES), 1) // HEAD
    for line in range(4):
        total = jnp.zeros((LANES, LANES), F32)
        for place, slot in enumerate(slots[line * 4 : line * 4 + 4]):
            total = jnp.where(group == place, slot, total)
        back_ref[pl.ds(TILES + line, LANES, stride=BACK), :] = total
    out_ref[...] = back_ref[...].astype(BF16)


def unpack_kernel(
    back_ref, values_ref, query_x_ref, key_x_ref, query_y_ref, key_y_ref, rows_ref, frame_ref
):
    rows_ref[...] = back_ref[...].astype(F32)
    for u in range(YU):
        for r in range(XR):
            tile = rows_ref[pl.ds(u * XR + r, LANES, stride=BACK), :]
            frame_ref[pl.ds(r * YU * LANES + u, LANES, stride=YU), :] = tile.T
    values_ref[...] = frame_ref[...].astype(BF16).reshape(values_ref.shape)
    source = lax.broadcasted_iota(jnp.int32, (LANES, 4 * LANES), 0)
    lane = lax.broadcasted_iota(jnp.int32, (LANES, 4 * LANES), 1)
    spread = (source == (lane // LANES) * HEAD + lane % HEAD).astype(BF16)
    own = source // HEAD == (lane % LANES) // HEAD
    sums = []
    for line in range(3):
        shares = rows_ref[pl.ds(TILES + line, LANES, stride=BACK), :].astype(BF16)
        total = jnp.sum(jnp.where(own, dot(shares, spread), 0.0), axis=0, keepdims=True)
        sums += [total[:, k * LANES : (k + 1) * LANES] for k in range(4)]
    for r in range(XR):
        query_x_ref[r : r + 1, :] = sums[r]
        key_x_ref[r : r + 1, :] = sums[XR + r]
    for u in range(YU):
        query_y_ref[u : u + 1, :] = sums[2 * XR + u]
        key_y_ref[u : u + 1, :] = sums[2 * XR + YU + u]


def shape(*dims, dtype=F32):
    return jax.ShapeDtypeStruct(dims, dtype)


def exchange(rows, count):
    parts = rows.reshape(LANES, count // 2, 2, LANES)
    moved = lax.all_to_all(parts, "slab", split_axis=0, concat_axis=0, tiled=True)
    return moved.reshape(LANES * count, LANES)


def on_device(grad_out, cached, values, query_x, key_x, query_y, key_y):
    nx, ny = XR * LANES, YU * LANES
    packed = pl.pallas_call(
        pack_kernel,
        out_shape=shape(SEND * LANES, LANES, dtype=BF16),
        scratch_shapes=[pltpu.VMEM((TILES * LANES, LANES), F32), pltpu.VMEM((SEND * LANES, LANES), F32)],
    )(grad_out, cached.transpose(1, 0, 2), values)
    fields = exchange(packed, SEND)
    kernels = pl.pallas_call(
        softmax_kernel,
        out_shape=(
            shape(nx, nx),
            shape(nx, nx, dtype=BF16),
            shape(ny, ny),
            shape(ny, ny, dtype=BF16),
            shape(nx, LANES, dtype=BF16),
            shape(nx, LANES, dtype=BF16),
            shape(ny, LANES, dtype=BF16),
            shape(ny, LANES, dtype=BF16),
        ),
        scratch_shapes=[pltpu.VMEM((ny, LANES), F32)],
    )(query_x, key_x, query_y, key_y)
    back = pl.pallas_call(
        channel_kernel,
        out_shape=shape(BACK * LANES, LANES, dtype=BF16),
        scratch_shapes=[pltpu.VMEM((SEND * LANES, LANES), F32), pltpu.VMEM((BACK * LANES, LANES), F32)],
    )(fields, *kernels)
    shares = exchange(back, BACK)
    return pl.pallas_call(
        unpack_kernel,
        out_shape=(
            shape(XR, ny, LANES, dtype=BF16),
            shape(XR, LANES),
            shape(XR, LANES),
            shape(YU, LANES),
            shape(YU, LANES),
        ),
        scratch_shapes=[pltpu.VMEM((BACK * LANES, LANES), F32), pltpu.VMEM((TILES * LANES, LANES), F32)],
    )(shares)


def solution(mesh):
    return jax.shard_map(
        on_device,
        mesh=mesh,
        in_specs=(
            P(("traj", "slab"), None, None),
            P("traj", "slab", None),
            P(("traj", "slab"), None, None),
            P("traj", None),
            P("traj", None),
            P("traj", None),
            P("traj", None),
        ),
        out_specs=(
            P(("traj", "slab"), None, None),
            P(("traj", "slab"), None),
            P(("traj", "slab"), None),
            P(("traj", "slab"), None),
            P(("traj", "slab"), None),
        ),
        check_vma=False,
    )
```

```python
import functools
import math

import jax
import jax.numpy as jnp
from jax import lax
from jax.experimental import pallas as pl
from jax.experimental.pallas import tpu as pltpu
from jax.sharding import PartitionSpec as P

HEAD = 32
LANES = 128
XR = 2
YU = 3
TILES = XR * YU
SEND = 3 * TILES
BACK = TILES + 4
F32 = jnp.float32
BF16 = jnp.bfloat16
ROOT = math.sqrt(HEAD)


def dot(a, b, dims=((1,), (0,))):
    return lax.dot_general(a, b, (dims, ((), ())), preferred_element_type=F32)


def pack_kernel(grad_ref, cached_ref, values_ref, out_ref, rows_ref, send_ref):
    for part, ref in enumerate((grad_ref, cached_ref, values_ref)):
        rows_ref[...] = ref[...].reshape(TILES * LANES, LANES).astype(F32)
        for u in range(YU):
            for r in range(XR):
                if part == 1:
                    tile = rows_ref[pl.ds(u * XR * LANES + r, LANES, stride=XR), :]
                else:
                    tile = rows_ref[pl.ds(r * YU * LANES + u, LANES, stride=YU), :]
                send_ref[pl.ds(part * TILES + u * XR + r, LANES, stride=SEND), :] = tile.T
    out_ref[...] = send_ref[...].astype(BF16)


def softmax_kernel(
    query_x_ref, key_x_ref, query_y_ref, key_y_ref,
    kernel_x_ref, kernel_xt_ref, kernel_y_ref, low_y_ref,
    tiled_qx_ref, tiled_kx_ref, tiled_qy_ref, tiled_ky_ref,
    rows_ref,
):
    head = lax.axis_index("slab") // HEAD
    source = lax.broadcasted_iota(jnp.int32, (LANES, LANES), 0)
    lane = lax.broadcasted_iota(jnp.int32, (LANES, LANES), 1)
    spread = (source == head * HEAD + lane % HEAD).astype(BF16)

    def permuted(ref, step):
        rows_ref[0 : step * LANES, :] = ref[...].astype(F32)
        return jnp.concatenate(
            [rows_ref[pl.ds(r, LANES, stride=step), :] for r in range(step)], axis=0
        ).astype(BF16)

    def softmax(tiled_q, tiled_k):
        first = lax.broadcasted_iota(jnp.int32, tiled_q.shape, 1) < HEAD
        scores = dot(jnp.where(first, tiled_q, 0), tiled_k, ((1,), (1,))) / ROOT
        top = jnp.max(scores, axis=1, keepdims=True)
        power = jnp.exp(scores - top)
        return power / jnp.sum(power, axis=1, keepdims=True)

    tiled_qx = dot(permuted(query_x_ref, XR), spread).astype(BF16)
    tiled_kx = dot(permuted(key_x_ref, XR), spread).astype(BF16)
    tiled_qy = dot(permuted(query_y_ref, YU), spread).astype(BF16)
    tiled_ky = dot(permuted(key_y_ref, YU), spread).astype(BF16)
    kernel_x = softmax(tiled_qx, tiled_kx)
    kernel_y = softmax(tiled_qy, tiled_ky)
    kernel_x_ref[...] = kernel_x
    kernel_xt_ref[...] = kernel_x.T.astype(BF16)
    kernel_y_ref[...] = kernel_y
    low_y_ref[...] = kernel_y.astype(BF16)
    tiled_qx_ref[...] = tiled_qx
    tiled_kx_ref[...] = tiled_kx
    tiled_qy_ref[...] = tiled_qy
    tiled_ky_ref[...] = tiled_ky


def channel_kernel(
    field_ref,
    kernel_x_ref, kernel_xt_ref, kernel_y_ref, low_y_ref,
    tiled_qx_ref, tiled_kx_ref, tiled_qy_ref, tiled_ky_ref,
    out_ref, rows_ref, back_ref,
):
    rows_ref[...] = field_ref[...].astype(F32)

    def tile(q):
        return rows_ref[pl.ds(q, LANES, stride=SEND), :].astype(BF16)

    def field(part):
        return jnp.concatenate(
            [
                jnp.concatenate([tile(part * TILES + u * XR + r) for u in range(YU)], axis=1)
                for r in range(XR)
            ],
            axis=0,
        )

    grad = field(0)
    values = field(2)
    cached = jnp.concatenate(
        [
            jnp.concatenate([tile(TILES + u * XR + r) for r in range(XR)], axis=1)
            for u in range(YU)
        ],
        axis=0,
    )
    mixed = dot(kernel_xt_ref[...], grad).astype(BF16)
    grad_values = dot(mixed, low_y_ref[...])
    for u in range(YU):
        for r in range(XR):
            back_ref[pl.ds(u * XR + r, LANES, stride=BACK), :] = grad_values[
                r * LANES : (r + 1) * LANES, u * LANES : (u + 1) * LANES
            ]

    def factor_grads(kernel, coupling, tiled_q, tiled_k):
        delta = jnp.sum(kernel * coupling, axis=1, keepdims=True)
        weighted = kernel * (coupling - delta) / ROOT
        high = weighted.astype(BF16)
        low = (weighted - high.astype(F32)).astype(BF16)
        grad_query = dot(high, tiled_k) + dot(low, tiled_k)
        grad_key = dot(high, tiled_q, ((0,), (0,))) + dot(low, tiled_q, ((0,), (0,)))
        return grad_query, grad_key

    query_x, key_x = factor_grads(
        kernel_x_ref[...], dot(grad, cached), tiled_qx_ref[...], tiled_kx_ref[...]
    )
    query_y, key_y = factor_grads(
        kernel_y_ref[...], dot(mixed, values, ((0,), (0,))), tiled_qy_ref[...], tiled_ky_ref[...]
    )
    slots = [query_x[r * LANES : (r + 1) * LANES] for r in range(XR)]
    slots += [key_x[r * LANES : (r + 1) * LANES] for r in range(XR)]
    slots += [query_y[u * LANES : (u + 1) * LANES] for u in range(YU)]
    slots += [key_y[u * LANES : (u + 1) * LANES] for u in range(YU)]
    group = lax.broadcasted_iota(jnp.int32, (LANES, LANES), 1) // HEAD
    for line in range(4):
        total = jnp.zeros((LANES, LANES), F32)
        for place, slot in enumerate(slots[line * 4 : line * 4 + 4]):
            total = jnp.where(group == place, slot, total)
        back_ref[pl.ds(TILES + line, LANES, stride=BACK), :] = total
    out_ref[...] = back_ref[...].astype(BF16)


def unpack_kernel(
    back_ref, values_ref, query_x_ref, key_x_ref, query_y_ref, key_y_ref, rows_ref, frame_ref
):
    rows_ref[...] = back_ref[...].astype(F32)
    for u in range(YU):
        for r in range(XR):
            tile = rows_ref[pl.ds(u * XR + r, LANES, stride=BACK), :]
            frame_ref[pl.ds(r * YU * LANES + u, LANES, stride=YU), :] = tile.T
    values_ref[...] = frame_ref[...].astype(BF16).reshape(values_ref.shape)
    source = lax.broadcasted_iota(jnp.int32, (LANES, 4 * LANES), 0)
    lane = lax.broadcasted_iota(jnp.int32, (LANES, 4 * LANES), 1)
    spread = (source == (lane // LANES) * HEAD + lane % HEAD).astype(BF16)
    own = source // HEAD == (lane % LANES) // HEAD
    sums = []
    for line in range(3):
        shares = rows_ref[pl.ds(TILES + line, LANES, stride=BACK), :].astype(BF16)
        total = jnp.sum(jnp.where(own, dot(shares, spread), 0.0), axis=0, keepdims=True)
        sums += [total[:, k * LANES : (k + 1) * LANES] for k in range(4)]
    for r in range(XR):
        query_x_ref[r : r + 1, :] = sums[r]
        key_x_ref[r : r + 1, :] = sums[XR + r]
    for u in range(YU):
        query_y_ref[u : u + 1, :] = sums[2 * XR + u]
        key_y_ref[u : u + 1, :] = sums[2 * XR + YU + u]


def shape(*dims, dtype=F32):
    return jax.ShapeDtypeStruct(dims, dtype)


def on_chip(array):
    return pltpu.with_memory_space_constraint(array, pltpu.VMEM)


def exchange(rows, count):
    parts = rows.reshape(LANES, count // 2, 2, LANES)
    moved = lax.all_to_all(parts, "slab", split_axis=0, concat_axis=0, tiled=True)
    return moved.reshape(LANES * count, LANES)


def on_device(grad_out, cached, values, query_x, key_x, query_y, key_y):
    nx, ny = XR * LANES, YU * LANES
    packed = pl.pallas_call(
        pack_kernel,
        out_shape=pltpu.VMEM((SEND * LANES, LANES), BF16),
        scratch_shapes=[pltpu.VMEM((TILES * LANES, LANES), F32), pltpu.VMEM((SEND * LANES, LANES), F32)],
    )(grad_out, cached.transpose(1, 0, 2), values)
    fields = exchange(packed, SEND)
    kernels = pl.pallas_call(
        softmax_kernel,
        out_shape=(
            pltpu.VMEM((nx, nx), F32),
            pltpu.VMEM((nx, nx), BF16),
            pltpu.VMEM((ny, ny), F32),
            pltpu.VMEM((ny, ny), BF16),
            pltpu.VMEM((nx, LANES), BF16),
            pltpu.VMEM((nx, LANES), BF16),
            pltpu.VMEM((ny, LANES), BF16),
            pltpu.VMEM((ny, LANES), BF16),
        ),
        scratch_shapes=[pltpu.VMEM((ny, LANES), F32)],
    )(query_x, key_x, query_y, key_y)
    back = pl.pallas_call(
        channel_kernel,
        out_shape=pltpu.VMEM((BACK * LANES, LANES), BF16),
        scratch_shapes=[pltpu.VMEM((SEND * LANES, LANES), F32), pltpu.VMEM((BACK * LANES, LANES), F32)],
    )(*map(on_chip, (fields, *kernels)))
    shares = exchange(back, BACK)
    return pl.pallas_call(
        unpack_kernel,
        out_shape=(
            shape(XR, ny, LANES, dtype=BF16),
            shape(XR, LANES),
            shape(XR, LANES),
            shape(YU, LANES),
            shape(YU, LANES),
        ),
        scratch_shapes=[pltpu.VMEM((BACK * LANES, LANES), F32), pltpu.VMEM((TILES * LANES, LANES), F32)],
    )(on_chip(shares))


def solution(mesh):
    return jax.shard_map(
        on_device,
        mesh=mesh,
        in_specs=(
            P(("traj", "slab"), None, None),
            P("traj", "slab", None),
            P(("traj", "slab"), None, None),
            P("traj", None),
            P("traj", None),
            P("traj", None),
            P("traj", None),
        ),
        out_specs=(
            P(("traj", "slab"), None, None),
            P(("traj", "slab"), None),
            P(("traj", "slab"), None),
            P(("traj", "slab"), None),
            P(("traj", "slab"), None),
        ),
        check_vma=False,
    )
```

```python
import functools
import math

import jax
import jax.numpy as jnp
from jax import lax
from jax.experimental import pallas as pl
from jax.experimental.pallas import tpu as pltpu
from jax.sharding import PartitionSpec as P

HEAD = 32
LANES = 128
XR = 2
YU = 3
TILES = XR * YU
SEND = 3 * TILES
BACK = TILES + 4
Z, Y, CORES = 8, 8, 2
F32 = jnp.float32
BF16 = jnp.bfloat16
ROOT = math.sqrt(HEAD)


def dot(a, b, dims=((1,), (0,))):
    return lax.dot_general(a, b, (dims, ((), ())), preferred_element_type=F32)


def owner(p):
    z, core, y = Z - 1 - p // (Y * CORES), CORES - 1 - p // Y % CORES, Y - 1 - p % Y
    return (z * Y + y) * CORES + core


def place(s):
    z, y, core = s // (Y * CORES), s // CORES % Y, s % CORES
    return ((Z - 1 - z) * CORES + CORES - 1 - core) * Y + Y - 1 - y


def pack_kernel(grad_ref, cached_ref, values_ref, out_ref, rows_ref, send_ref):
    for part, ref in enumerate((grad_ref, cached_ref, values_ref)):
        rows_ref[...] = ref[...].reshape(TILES * LANES, LANES).astype(F32)
        for u in range(YU):
            for r in range(XR):
                if part == 1:
                    tile = rows_ref[pl.ds(u * XR * LANES + r, LANES, stride=XR), :]
                else:
                    tile = rows_ref[pl.ds(r * YU * LANES + u, LANES, stride=YU), :]
                send_ref[pl.ds(part * TILES + u * XR + r, LANES, stride=SEND), :] = tile.T
    out_ref[...] = send_ref[...].astype(BF16)


def softmax_kernel(
    query_x_ref, key_x_ref, query_y_ref, key_y_ref,
    kernel_x_ref, kernel_xt_ref, kernel_y_ref, low_y_ref,
    tiled_qx_ref, tiled_kx_ref, tiled_qy_ref, tiled_ky_ref, natural_ref, placed_ref,
    rows_ref,
):
    head = place(lax.axis_index("slab")) // HEAD
    source = lax.broadcasted_iota(jnp.int32, (LANES, LANES), 0)
    lane = lax.broadcasted_iota(jnp.int32, (LANES, LANES), 1)
    spread = (source == head * HEAD + lane % HEAD).astype(BF16)

    natural = (source == owner(lane)).astype(BF16)
    placed = (owner(source) == lane).astype(BF16)

    def put(rows):
        blocks = [dot(placed, rows[i : i + LANES]) for i in range(0, rows.shape[0], LANES)]
        return jnp.concatenate(blocks, axis=0).astype(BF16)

    def permuted(ref, step):
        rows_ref[0 : step * LANES, :] = ref[...].astype(F32)
        return jnp.concatenate(
            [rows_ref[pl.ds(r, LANES, stride=step), :] for r in range(step)], axis=0
        ).astype(BF16)

    def softmax(tiled_q, tiled_k):
        first = lax.broadcasted_iota(jnp.int32, tiled_q.shape, 1) < HEAD
        scores = dot(jnp.where(first, tiled_q, 0), tiled_k, ((1,), (1,))) / ROOT
        top = jnp.max(scores, axis=1, keepdims=True)
        power = jnp.exp(scores - top)
        return power / jnp.sum(power, axis=1, keepdims=True)

    tiled_qx = dot(put(permuted(query_x_ref, XR)), spread).astype(BF16)
    tiled_kx = dot(permuted(key_x_ref, XR), spread).astype(BF16)
    tiled_qy = dot(permuted(query_y_ref, YU), spread).astype(BF16)
    tiled_ky = dot(permuted(key_y_ref, YU), spread).astype(BF16)
    kernel_x = softmax(tiled_qx, tiled_kx)
    kernel_y = softmax(tiled_qy, tiled_ky)
    kernel_x_ref[...] = kernel_x
    kernel_xt_ref[...] = put(kernel_x.T.astype(BF16))
    kernel_y_ref[...] = kernel_y
    low_y_ref[...] = kernel_y.astype(BF16)
    tiled_qx_ref[...] = tiled_qx
    tiled_kx_ref[...] = tiled_kx
    tiled_qy_ref[...] = tiled_qy
    tiled_ky_ref[...] = tiled_ky
    natural_ref[...] = natural
    placed_ref[...] = placed


def channel_kernel(
    field_ref,
    kernel_x_ref, kernel_xt_ref, kernel_y_ref, low_y_ref,
    tiled_qx_ref, tiled_kx_ref, tiled_qy_ref, tiled_ky_ref, natural_ref, placed_ref,
    out_ref, rows_ref, back_ref,
):
    rows_ref[...] = field_ref[...].astype(F32)

    def tile(q):
        return rows_ref[pl.ds(q, LANES, stride=SEND), :].astype(BF16)

    def field(part):
        return jnp.concatenate(
            [
                jnp.concatenate([tile(part * TILES + u * XR + r) for u in range(YU)], axis=1)
                for r in range(XR)
            ],
            axis=0,
        )

    grad = field(0)
    values = field(2)
    cached = jnp.concatenate([tile(TILES + q) for q in range(TILES)], axis=1)
    cached = dot(natural_ref[...], cached).astype(BF16)
    cached = jnp.concatenate(
        [cached[:, u * XR * LANES : (u + 1) * XR * LANES] for u in range(YU)], axis=0
    )
    mixed = dot(kernel_xt_ref[...], grad).astype(BF16)
    grad_values = dot(mixed, low_y_ref[...])
    for u in range(YU):
        for r in range(XR):
            back_ref[pl.ds(u * XR + r, LANES, stride=BACK), :] = grad_values[
                r * LANES : (r + 1) * LANES, u * LANES : (u + 1) * LANES
            ]

    def factor_grads(kernel, coupling, tiled_q, tiled_k):
        delta = jnp.sum(kernel * coupling, axis=1, keepdims=True)
        weighted = kernel * (coupling - delta) / ROOT
        high = weighted.astype(BF16)
        low = (weighted - high.astype(F32)).astype(BF16)
        grad_query = dot(high, tiled_k) + dot(low, tiled_k)
        grad_key = dot(high, tiled_q, ((0,), (0,))) + dot(low, tiled_q, ((0,), (0,)))
        return grad_query, grad_key

    query_x, key_x = factor_grads(
        kernel_x_ref[...], dot(grad, cached), tiled_qx_ref[...], tiled_kx_ref[...]
    )
    query_y, key_y = factor_grads(
        kernel_y_ref[...], dot(mixed, values, ((0,), (0,))), tiled_qy_ref[...], tiled_ky_ref[...]
    )
    group = lax.broadcasted_iota(jnp.int32, (LANES, LANES), 1) // HEAD

    def line_up(slots):
        total = jnp.zeros((LANES, LANES), F32)
        for at, slot in slots:
            total = jnp.where(group == at, slot, total)
        return total

    slots = [key_x[r * LANES : (r + 1) * LANES] for r in range(XR)]
    slots += [query_y[u * LANES : (u + 1) * LANES] for u in range(YU)]
    slots += [key_y[u * LANES : (u + 1) * LANES] for u in range(YU)]
    lines = [line_up(zip((2, 3), slots[:2])), line_up(zip(range(4), slots[2:6])), line_up(zip((0, 1), slots[6:]))]
    lines = dot(placed_ref[...], jnp.concatenate(lines, axis=1).astype(BF16))
    first = line_up((r, query_x[r * LANES : (r + 1) * LANES]) for r in range(XR))
    back_ref[pl.ds(TILES, LANES, stride=BACK), :] = first + lines[:, :LANES]
    back_ref[pl.ds(TILES + 1, LANES, stride=BACK), :] = lines[:, LANES : 2 * LANES]
    back_ref[pl.ds(TILES + 2, LANES, stride=BACK), :] = lines[:, 2 * LANES :]
    back_ref[pl.ds(TILES + 3, LANES, stride=BACK), :] = jnp.zeros((LANES, LANES), F32)
    out_ref[...] = back_ref[...].astype(BF16)


def unpack_kernel(
    back_ref, values_ref, query_x_ref, key_x_ref, query_y_ref, key_y_ref, rows_ref, frame_ref
):
    rows_ref[...] = back_ref[...].astype(F32)
    for u in range(YU):
        for r in range(XR):
            tile = rows_ref[pl.ds(u * XR + r, LANES, stride=BACK), :]
            frame_ref[pl.ds(r * YU * LANES + u, LANES, stride=YU), :] = tile.T
    values_ref[...] = frame_ref[...].astype(BF16).reshape(values_ref.shape)
    source = lax.broadcasted_iota(jnp.int32, (LANES, 4 * LANES), 0)
    lane = lax.broadcasted_iota(jnp.int32, (LANES, 4 * LANES), 1)
    spread = (source == (lane // LANES) * HEAD + lane % HEAD).astype(BF16)
    own = source // HEAD == (lane % LANES) // HEAD
    sums = []
    for line in range(3):
        shares = rows_ref[pl.ds(TILES + line, LANES, stride=BACK), :].astype(BF16)
        total = jnp.sum(jnp.where(own, dot(shares, spread), 0.0), axis=0, keepdims=True)
        sums += [total[:, k * LANES : (k + 1) * LANES] for k in range(4)]
    for r in range(XR):
        query_x_ref[r : r + 1, :] = sums[r]
        key_x_ref[r : r + 1, :] = sums[XR + r]
    for u in range(YU):
        query_y_ref[u : u + 1, :] = sums[2 * XR + u]
        key_y_ref[u : u + 1, :] = sums[2 * XR + YU + u]


def shape(*dims, dtype=F32):
    return jax.ShapeDtypeStruct(dims, dtype)


def on_chip(array):
    return pltpu.with_memory_space_constraint(array, pltpu.VMEM)


def exchange(rows, count):
    parts = rows.reshape(LANES, count // 2, 2, LANES)
    order = [[owner(p) for p in range(LANES)]]
    moved = lax.all_to_all(
        parts, "slab", split_axis=0, concat_axis=0, tiled=True, axis_index_groups=order
    )
    return moved.reshape(LANES * count, LANES)


def on_device(grad_out, cached, values, query_x, key_x, query_y, key_y):
    nx, ny = XR * LANES, YU * LANES
    packed = pl.pallas_call(
        pack_kernel,
        out_shape=pltpu.VMEM((SEND * LANES, LANES), BF16),
        scratch_shapes=[pltpu.VMEM((TILES * LANES, LANES), F32), pltpu.VMEM((SEND * LANES, LANES), F32)],
    )(grad_out, cached.transpose(1, 0, 2), values)
    fields = exchange(packed, SEND)
    kernels = pl.pallas_call(
        softmax_kernel,
        out_shape=(
            pltpu.VMEM((nx, nx), F32),
            pltpu.VMEM((nx, nx), BF16),
            pltpu.VMEM((ny, ny), F32),
            pltpu.VMEM((ny, ny), BF16),
            pltpu.VMEM((nx, LANES), BF16),
            pltpu.VMEM((nx, LANES), BF16),
            pltpu.VMEM((ny, LANES), BF16),
            pltpu.VMEM((ny, LANES), BF16),
            pltpu.VMEM((LANES, LANES), BF16),
            pltpu.VMEM((LANES, LANES), BF16),
        ),
        scratch_shapes=[pltpu.VMEM((ny, LANES), F32)],
    )(query_x, key_x, query_y, key_y)
    back = pl.pallas_call(
        channel_kernel,
        out_shape=pltpu.VMEM((BACK * LANES, LANES), BF16),
        scratch_shapes=[pltpu.VMEM((SEND * LANES, LANES), F32), pltpu.VMEM((BACK * LANES, LANES), F32)],
    )(*map(on_chip, (fields, *kernels)))
    shares = exchange(back, BACK)
    return pl.pallas_call(
        unpack_kernel,
        out_shape=(
            shape(XR, ny, LANES, dtype=BF16),
            shape(XR, LANES),
            shape(XR, LANES),
            shape(YU, LANES),
            shape(YU, LANES),
        ),
        scratch_shapes=[pltpu.VMEM((BACK * LANES, LANES), F32), pltpu.VMEM((TILES * LANES, LANES), F32)],
    )(on_chip(shares))


def solution(mesh):
    return jax.shard_map(
        on_device,
        mesh=mesh,
        in_specs=(
            P(("traj", "slab"), None, None),
            P("traj", "slab", None),
            P(("traj", "slab"), None, None),
            P("traj", None),
            P("traj", None),
            P("traj", None),
            P("traj", None),
        ),
        out_specs=(
            P(("traj", "slab"), None, None),
            P(("traj", "slab"), None),
            P(("traj", "slab"), None),
            P(("traj", "slab"), None),
            P(("traj", "slab"), None),
        ),
        check_vma=False,
    )
```

```python
import functools
import math

import jax
import jax.numpy as jnp
from jax import lax
from jax.experimental import pallas as pl
from jax.experimental.pallas import tpu as pltpu
from jax.sharding import PartitionSpec as P

HEAD = 32
LANES = 128
XR = 2
YU = 3
TILES = XR * YU
SEND = 3 * TILES
BACK = TILES + 4
Z, Y, CORES = 8, 8, 2
FIRST = (5, 4)
F32 = jnp.float32
BF16 = jnp.bfloat16
ROOT = math.sqrt(HEAD)


def dot(a, b, dims=((1,), (0,))):
    return lax.dot_general(a, b, (dims, ((), ())), preferred_element_type=F32)


def owner(p):
    z = (Z + FIRST[0] - p // (Y * CORES)) % Z
    y = (Y + FIRST[1] - p % Y) % Y
    return (z * Y + y) * CORES + CORES - 1 - p // Y % CORES


def place(s):
    z = (Z + FIRST[0] - s // (Y * CORES)) % Z
    y = (Y + FIRST[1] - s // CORES % Y) % Y
    return (z * CORES + CORES - 1 - s % CORES) * Y + y


def pack_kernel(grad_ref, cached_ref, values_ref, out_ref, rows_ref, send_ref):
    for part, ref in enumerate((grad_ref, cached_ref, values_ref)):
        rows_ref[...] = ref[...].reshape(TILES * LANES, LANES).astype(F32)
        for u in range(YU):
            for r in range(XR):
                if part == 1:
                    tile = rows_ref[pl.ds(u * XR * LANES + r, LANES, stride=XR), :]
                else:
                    tile = rows_ref[pl.ds(r * YU * LANES + u, LANES, stride=YU), :]
                send_ref[pl.ds(part * TILES + u * XR + r, LANES, stride=SEND), :] = tile.T
    out_ref[...] = send_ref[...].astype(BF16)


def softmax_kernel(
    query_x_ref, key_x_ref, query_y_ref, key_y_ref,
    kernel_x_ref, kernel_xt_ref, kernel_y_ref, low_y_ref,
    tiled_qx_ref, tiled_kx_ref, tiled_qy_ref, tiled_ky_ref, natural_ref, placed_ref,
    rows_ref,
):
    head = place(lax.axis_index("slab")) // HEAD
    source = lax.broadcasted_iota(jnp.int32, (LANES, LANES), 0)
    lane = lax.broadcasted_iota(jnp.int32, (LANES, LANES), 1)
    spread = (source == head * HEAD + lane % HEAD).astype(BF16)

    natural = (source == owner(lane)).astype(BF16)
    placed = (owner(source) == lane).astype(BF16)

    def put(rows):
        blocks = [dot(placed, rows[i : i + LANES]) for i in range(0, rows.shape[0], LANES)]
        return jnp.concatenate(blocks, axis=0).astype(BF16)

    def permuted(ref, step):
        rows_ref[0 : step * LANES, :] = ref[...].astype(F32)
        return jnp.concatenate(
            [rows_ref[pl.ds(r, LANES, stride=step), :] for r in range(step)], axis=0
        ).astype(BF16)

    def softmax(tiled_q, tiled_k):
        first = lax.broadcasted_iota(jnp.int32, tiled_q.shape, 1) < HEAD
        scores = dot(jnp.where(first, tiled_q, 0), tiled_k, ((1,), (1,))) / ROOT
        top = jnp.max(scores, axis=1, keepdims=True)
        power = jnp.exp(scores - top)
        return power / jnp.sum(power, axis=1, keepdims=True)

    tiled_qx = dot(put(permuted(query_x_ref, XR)), spread).astype(BF16)
    tiled_kx = dot(permuted(key_x_ref, XR), spread).astype(BF16)
    tiled_qy = dot(permuted(query_y_ref, YU), spread).astype(BF16)
    tiled_ky = dot(permuted(key_y_ref, YU), spread).astype(BF16)
    kernel_x = softmax(tiled_qx, tiled_kx)
    kernel_y = softmax(tiled_qy, tiled_ky)
    kernel_x_ref[...] = kernel_x
    kernel_xt_ref[...] = put(kernel_x.T.astype(BF16))
    kernel_y_ref[...] = kernel_y
    low_y_ref[...] = kernel_y.astype(BF16)
    tiled_qx_ref[...] = tiled_qx
    tiled_kx_ref[...] = tiled_kx
    tiled_qy_ref[...] = tiled_qy
    tiled_ky_ref[...] = tiled_ky
    natural_ref[...] = natural
    placed_ref[...] = placed


def channel_kernel(
    field_ref,
    kernel_x_ref, kernel_xt_ref, kernel_y_ref, low_y_ref,
    tiled_qx_ref, tiled_kx_ref, tiled_qy_ref, tiled_ky_ref, natural_ref, placed_ref,
    out_ref, rows_ref, back_ref,
):
    rows_ref[...] = field_ref[...].astype(F32)

    def tile(q):
        return rows_ref[pl.ds(q, LANES, stride=SEND), :].astype(BF16)

    def field(part):
        return jnp.concatenate(
            [
                jnp.concatenate([tile(part * TILES + u * XR + r) for u in range(YU)], axis=1)
                for r in range(XR)
            ],
            axis=0,
        )

    grad = field(0)
    values = field(2)
    cached = jnp.concatenate([tile(TILES + q) for q in range(TILES)], axis=1)
    cached = dot(natural_ref[...], cached).astype(BF16)
    cached = jnp.concatenate(
        [cached[:, u * XR * LANES : (u + 1) * XR * LANES] for u in range(YU)], axis=0
    )
    mixed = dot(kernel_xt_ref[...], grad).astype(BF16)
    grad_values = dot(mixed, low_y_ref[...])
    for u in range(YU):
        for r in range(XR):
            back_ref[pl.ds(u * XR + r, LANES, stride=BACK), :] = grad_values[
                r * LANES : (r + 1) * LANES, u * LANES : (u + 1) * LANES
            ]

    def factor_grads(kernel, coupling, tiled_q, tiled_k):
        delta = jnp.sum(kernel * coupling, axis=1, keepdims=True)
        weighted = kernel * (coupling - delta) / ROOT
        high = weighted.astype(BF16)
        low = (weighted - high.astype(F32)).astype(BF16)
        grad_query = dot(high, tiled_k) + dot(low, tiled_k)
        grad_key = dot(high, tiled_q, ((0,), (0,))) + dot(low, tiled_q, ((0,), (0,)))
        return grad_query, grad_key

    query_x, key_x = factor_grads(
        kernel_x_ref[...], dot(grad, cached), tiled_qx_ref[...], tiled_kx_ref[...]
    )
    query_y, key_y = factor_grads(
        kernel_y_ref[...], dot(mixed, values, ((0,), (0,))), tiled_qy_ref[...], tiled_ky_ref[...]
    )
    group = lax.broadcasted_iota(jnp.int32, (LANES, LANES), 1) // HEAD

    def line_up(slots):
        total = jnp.zeros((LANES, LANES), F32)
        for at, slot in slots:
            total = jnp.where(group == at, slot, total)
        return total

    slots = [key_x[r * LANES : (r + 1) * LANES] for r in range(XR)]
    slots += [query_y[u * LANES : (u + 1) * LANES] for u in range(YU)]
    slots += [key_y[u * LANES : (u + 1) * LANES] for u in range(YU)]
    lines = [line_up(zip((2, 3), slots[:2])), line_up(zip(range(4), slots[2:6])), line_up(zip((0, 1), slots[6:]))]
    lines = dot(placed_ref[...], jnp.concatenate(lines, axis=1).astype(BF16))
    first = line_up((r, query_x[r * LANES : (r + 1) * LANES]) for r in range(XR))
    back_ref[pl.ds(TILES, LANES, stride=BACK), :] = first + lines[:, :LANES]
    back_ref[pl.ds(TILES + 1, LANES, stride=BACK), :] = lines[:, LANES : 2 * LANES]
    back_ref[pl.ds(TILES + 2, LANES, stride=BACK), :] = lines[:, 2 * LANES :]
    back_ref[pl.ds(TILES + 3, LANES, stride=BACK), :] = jnp.zeros((LANES, LANES), F32)
    out_ref[...] = back_ref[...].astype(BF16)


def unpack_kernel(
    back_ref, values_ref, query_x_ref, key_x_ref, query_y_ref, key_y_ref, rows_ref, frame_ref
):
    rows_ref[...] = back_ref[...].astype(F32)
    for u in range(YU):
        for r in range(XR):
            tile = rows_ref[pl.ds(u * XR + r, LANES, stride=BACK), :]
            frame_ref[pl.ds(r * YU * LANES + u, LANES, stride=YU), :] = tile.T
    values_ref[...] = frame_ref[...].astype(BF16).reshape(values_ref.shape)
    source = lax.broadcasted_iota(jnp.int32, (LANES, 4 * LANES), 0)
    lane = lax.broadcasted_iota(jnp.int32, (LANES, 4 * LANES), 1)
    spread = (source == (lane // LANES) * HEAD + lane % HEAD).astype(BF16)
    own = source // HEAD == (lane % LANES) // HEAD
    sums = []
    for line in range(3):
        shares = rows_ref[pl.ds(TILES + line, LANES, stride=BACK), :].astype(BF16)
        total = jnp.sum(jnp.where(own, dot(shares, spread), 0.0), axis=0, keepdims=True)
        sums += [total[:, k * LANES : (k + 1) * LANES] for k in range(4)]
    for r in range(XR):
        query_x_ref[r : r + 1, :] = sums[r]
        key_x_ref[r : r + 1, :] = sums[XR + r]
    for u in range(YU):
        query_y_ref[u : u + 1, :] = sums[2 * XR + u]
        key_y_ref[u : u + 1, :] = sums[2 * XR + YU + u]


def shape(*dims, dtype=F32):
    return jax.ShapeDtypeStruct(dims, dtype)


def on_chip(array):
    return pltpu.with_memory_space_constraint(array, pltpu.VMEM)


def exchange(rows, count):
    parts = rows.reshape(LANES, count // 2, 2, LANES)
    order = [[owner(p) for p in range(LANES)]]
    moved = lax.all_to_all(
        parts, "slab", split_axis=0, concat_axis=0, tiled=True, axis_index_groups=order
    )
    return moved.reshape(LANES * count, LANES)


def on_device(grad_out, cached, values, query_x, key_x, query_y, key_y):
    nx, ny = XR * LANES, YU * LANES
    packed = pl.pallas_call(
        pack_kernel,
        out_shape=pltpu.VMEM((SEND * LANES, LANES), BF16),
        scratch_shapes=[pltpu.VMEM((TILES * LANES, LANES), F32), pltpu.VMEM((SEND * LANES, LANES), F32)],
    )(grad_out, cached.transpose(1, 0, 2), values)
    fields = exchange(packed, SEND)
    kernels = pl.pallas_call(
        softmax_kernel,
        out_shape=(
            pltpu.VMEM((nx, nx), F32),
            pltpu.VMEM((nx, nx), BF16),
            pltpu.VMEM((ny, ny), F32),
            pltpu.VMEM((ny, ny), BF16),
            pltpu.VMEM((nx, LANES), BF16),
            pltpu.VMEM((nx, LANES), BF16),
            pltpu.VMEM((ny, LANES), BF16),
            pltpu.VMEM((ny, LANES), BF16),
            pltpu.VMEM((LANES, LANES), BF16),
            pltpu.VMEM((LANES, LANES), BF16),
        ),
        scratch_shapes=[pltpu.VMEM((ny, LANES), F32)],
    )(query_x, key_x, query_y, key_y)
    back = pl.pallas_call(
        channel_kernel,
        out_shape=pltpu.VMEM((BACK * LANES, LANES), BF16),
        scratch_shapes=[pltpu.VMEM((SEND * LANES, LANES), F32), pltpu.VMEM((BACK * LANES, LANES), F32)],
    )(*map(on_chip, (fields, *kernels)))
    shares = exchange(back, BACK)
    return pl.pallas_call(
        unpack_kernel,
        out_shape=(
            shape(XR, ny, LANES, dtype=BF16),
            shape(XR, LANES),
            shape(XR, LANES),
            shape(YU, LANES),
            shape(YU, LANES),
        ),
        scratch_shapes=[pltpu.VMEM((BACK * LANES, LANES), F32), pltpu.VMEM((TILES * LANES, LANES), F32)],
    )(on_chip(shares))


def solution(mesh):
    return jax.shard_map(
        on_device,
        mesh=mesh,
        in_specs=(
            P(("traj", "slab"), None, None),
            P("traj", "slab", None),
            P(("traj", "slab"), None, None),
            P("traj", None),
            P("traj", None),
            P("traj", None),
            P("traj", None),
        ),
        out_specs=(
            P(("traj", "slab"), None, None),
            P(("traj", "slab"), None),
            P(("traj", "slab"), None),
            P(("traj", "slab"), None),
            P(("traj", "slab"), None),
        ),
        check_vma=False,
    )
```

```python
import functools
import math

import jax
import jax.numpy as jnp
from jax import lax
from jax.experimental import pallas as pl
from jax.experimental.pallas import tpu as pltpu
from jax.sharding import PartitionSpec as P

HEAD = 32
LANES = 128
XR = 2
YU = 3
TILES = XR * YU
SEND = 3 * TILES
BACK = TILES + 4
Z, Y, CORES = 8, 8, 2
FIRST = (5, 4)
F32 = jnp.float32
BF16 = jnp.bfloat16
ROOT = math.sqrt(HEAD)


def dot(a, b, dims=((1,), (0,))):
    return lax.dot_general(a, b, (dims, ((), ())), preferred_element_type=F32)


def owner(p):
    z = (Z + FIRST[0] - p // (Y * CORES)) % Z
    y = (Y + FIRST[1] - p % Y) % Y
    return (z * Y + y) * CORES + CORES - 1 - p // Y % CORES


def place(s):
    z = (Z + FIRST[0] - s // (Y * CORES)) % Z
    y = (Y + FIRST[1] - s // CORES % Y) % Y
    return (z * CORES + CORES - 1 - s % CORES) * Y + y


def entry_kernel(
    grad_ref, cached_ref, values_ref, query_x_ref, key_x_ref, query_y_ref, key_y_ref,
    out_ref, tiled_qx_ref, tiled_kx_ref, placed_kx_ref, tiled_qy_ref, tiled_ky_ref, natural_ref, placed_ref,
    rows_ref, send_ref, factor_ref,
):
    for part, ref in enumerate((grad_ref, cached_ref, values_ref)):
        rows_ref[part] = ref[...].reshape(TILES * LANES, LANES).astype(F32)
        for u in range(YU):
            for r in range(XR):
                if part == 1:
                    tile = rows_ref[part, pl.ds(u * XR * LANES + r, LANES, stride=XR), :]
                else:
                    tile = rows_ref[part, pl.ds(r * YU * LANES + u, LANES, stride=YU), :]
                send_ref[pl.ds(part * TILES + u * XR + r, LANES, stride=SEND), :] = tile.T
    out_ref[...] = send_ref[...].astype(BF16)

    head = place(lax.axis_index("slab")) // HEAD
    source = lax.broadcasted_iota(jnp.int32, (LANES, LANES), 0)
    lane = lax.broadcasted_iota(jnp.int32, (LANES, LANES), 1)
    spread = (source == head * HEAD + lane % HEAD).astype(BF16)
    placed = (owner(source) == lane).astype(BF16)
    natural_ref[...] = (source == owner(lane)).astype(BF16)
    placed_ref[...] = placed

    def tiled(at, ref, step):
        factor_ref[at, 0 : step * LANES, :] = dot(ref[...], spread)
        blocks = [factor_ref[at, pl.ds(r, LANES, stride=step), :] for r in range(step)]
        return [block.astype(BF16) for block in blocks]

    def put(blocks):
        return jnp.concatenate([dot(placed, block) for block in blocks], axis=0).astype(BF16)

    query_x = tiled(0, query_x_ref, XR)
    key_x = tiled(1, key_x_ref, XR)
    tiled_qx_ref[...] = put(query_x)
    placed_kx_ref[...] = put(key_x)
    tiled_kx_ref[...] = jnp.concatenate(key_x, axis=0)
    tiled_qy_ref[...] = jnp.concatenate(tiled(2, query_y_ref, YU), axis=0)
    tiled_ky_ref[...] = jnp.concatenate(tiled(3, key_y_ref, YU), axis=0)


def softmax(tiled_q, tiled_k, axis):
    first = lax.broadcasted_iota(jnp.int32, tiled_q.shape, 1) < HEAD
    scores = dot(jnp.where(first, tiled_q, 0), tiled_k, ((1,), (1,))) / ROOT
    power = jnp.exp(scores - jnp.max(scores, axis=axis, keepdims=True))
    return power / jnp.sum(power, axis=axis, keepdims=True)


def channel_kernel(
    field_ref, tiled_qx_ref, tiled_kx_ref, placed_kx_ref, tiled_qy_ref, tiled_ky_ref, natural_ref, placed_ref,
    out_ref, rows_ref, back_ref,
):
    rows_ref[...] = field_ref[...].astype(F32)

    def tile(q):
        return rows_ref[pl.ds(q, LANES, stride=SEND), :].astype(BF16)

    def field(part):
        return jnp.concatenate(
            [
                jnp.concatenate([tile(part * TILES + u * XR + r) for u in range(YU)], axis=1)
                for r in range(XR)
            ],
            axis=0,
        )

    grad = field(0)
    values = field(2)
    cached = jnp.concatenate([tile(TILES + q) for q in range(TILES)], axis=1)
    cached = dot(natural_ref[...], cached).astype(BF16)
    cached = jnp.concatenate(
        [cached[:, u * XR * LANES : (u + 1) * XR * LANES] for u in range(YU)], axis=0
    )
    kernel_x = softmax(tiled_qx_ref[...], tiled_kx_ref[...], 1)
    kernel_xt = softmax(placed_kx_ref[...], tiled_qx_ref[...], 0)
    kernel_y = softmax(tiled_qy_ref[...], tiled_ky_ref[...], 1)
    mixed = dot(kernel_xt.astype(BF16), grad).astype(BF16)
    grad_values = dot(mixed, kernel_y.astype(BF16))
    for u in range(YU):
        for r in range(XR):
            back_ref[pl.ds(u * XR + r, LANES, stride=BACK), :] = grad_values[
                r * LANES : (r + 1) * LANES, u * LANES : (u + 1) * LANES
            ]

    def factor_grads(kernel, coupling, tiled_q, tiled_k):
        delta = jnp.sum(kernel * coupling, axis=1, keepdims=True)
        weighted = kernel * (coupling - delta) / ROOT
        high = weighted.astype(BF16)
        low = (weighted - high.astype(F32)).astype(BF16)
        grad_query = dot(high, tiled_k) + dot(low, tiled_k)
        grad_key = dot(high, tiled_q, ((0,), (0,))) + dot(low, tiled_q, ((0,), (0,)))
        return grad_query, grad_key

    query_x, key_x = factor_grads(
        kernel_x, dot(grad, cached), tiled_qx_ref[...], tiled_kx_ref[...]
    )
    query_y, key_y = factor_grads(
        kernel_y, dot(mixed, values, ((0,), (0,))), tiled_qy_ref[...], tiled_ky_ref[...]
    )
    group = lax.broadcasted_iota(jnp.int32, (LANES, LANES), 1) // HEAD

    def line_up(slots):
        total = jnp.zeros((LANES, LANES), F32)
        for at, slot in slots:
            total = jnp.where(group == at, slot, total)
        return total

    slots = [key_x[r * LANES : (r + 1) * LANES] for r in range(XR)]
    slots += [query_y[u * LANES : (u + 1) * LANES] for u in range(YU)]
    slots += [key_y[u * LANES : (u + 1) * LANES] for u in range(YU)]
    lines = [line_up(zip((2, 3), slots[:2])), line_up(zip(range(4), slots[2:6])), line_up(zip((0, 1), slots[6:]))]
    lines = dot(placed_ref[...], jnp.concatenate(lines, axis=1).astype(BF16))
    first = line_up((r, query_x[r * LANES : (r + 1) * LANES]) for r in range(XR))
    back_ref[pl.ds(TILES, LANES, stride=BACK), :] = first + lines[:, :LANES]
    back_ref[pl.ds(TILES + 1, LANES, stride=BACK), :] = lines[:, LANES : 2 * LANES]
    back_ref[pl.ds(TILES + 2, LANES, stride=BACK), :] = lines[:, 2 * LANES :]
    back_ref[pl.ds(TILES + 3, LANES, stride=BACK), :] = jnp.zeros((LANES, LANES), F32)
    out_ref[...] = back_ref[...].astype(BF16)


def unpack_kernel(
    back_ref, values_ref, query_x_ref, key_x_ref, query_y_ref, key_y_ref, rows_ref, frame_ref
):
    rows_ref[...] = back_ref[...].astype(F32)
    for u in range(YU):
        for r in range(XR):
            tile = rows_ref[pl.ds(u * XR + r, LANES, stride=BACK), :]
            frame_ref[pl.ds(r * YU * LANES + u, LANES, stride=YU), :] = tile.T
    values_ref[...] = frame_ref[...].astype(BF16).reshape(values_ref.shape)
    source = lax.broadcasted_iota(jnp.int32, (LANES, 4 * LANES), 0)
    lane = lax.broadcasted_iota(jnp.int32, (LANES, 4 * LANES), 1)
    spread = (source == (lane // LANES) * HEAD + lane % HEAD).astype(BF16)
    own = source // HEAD == (lane % LANES) // HEAD
    sums = []
    for line in range(3):
        shares = rows_ref[pl.ds(TILES + line, LANES, stride=BACK), :].astype(BF16)
        total = jnp.sum(jnp.where(own, dot(shares, spread), 0.0), axis=0, keepdims=True)
        sums += [total[:, k * LANES : (k + 1) * LANES] for k in range(4)]
    for r in range(XR):
        query_x_ref[r : r + 1, :] = sums[r]
        key_x_ref[r : r + 1, :] = sums[XR + r]
    for u in range(YU):
        query_y_ref[u : u + 1, :] = sums[2 * XR + u]
        key_y_ref[u : u + 1, :] = sums[2 * XR + YU + u]


def shape(*dims, dtype=F32):
    return jax.ShapeDtypeStruct(dims, dtype)


def on_chip(array):
    return pltpu.with_memory_space_constraint(array, pltpu.VMEM)


def exchange(rows, count):
    parts = rows.reshape(LANES, count // 2, 2, LANES)
    order = [[owner(p) for p in range(LANES)]]
    moved = lax.all_to_all(
        parts, "slab", split_axis=0, concat_axis=0, tiled=True, axis_index_groups=order
    )
    return moved.reshape(LANES * count, LANES)


def on_device(grad_out, cached, values, query_x, key_x, query_y, key_y):
    nx, ny = XR * LANES, YU * LANES
    packed, *factors = pl.pallas_call(
        entry_kernel,
        out_shape=(
            pltpu.VMEM((SEND * LANES, LANES), BF16),
            pltpu.VMEM((nx, LANES), BF16),
            pltpu.VMEM((nx, LANES), BF16),
            pltpu.VMEM((nx, LANES), BF16),
            pltpu.VMEM((ny, LANES), BF16),
            pltpu.VMEM((ny, LANES), BF16),
            pltpu.VMEM((LANES, LANES), BF16),
            pltpu.VMEM((LANES, LANES), BF16),
        ),
        scratch_shapes=[
            pltpu.VMEM((3, TILES * LANES, LANES), F32),
            pltpu.VMEM((SEND * LANES, LANES), F32),
            pltpu.VMEM((4, ny, LANES), F32),
        ],
    )(grad_out, cached.transpose(1, 0, 2), values, query_x, key_x, query_y, key_y)
    fields = exchange(packed, SEND)
    back = pl.pallas_call(
        channel_kernel,
        out_shape=pltpu.VMEM((BACK * LANES, LANES), BF16),
        scratch_shapes=[pltpu.VMEM((SEND * LANES, LANES), F32), pltpu.VMEM((BACK * LANES, LANES), F32)],
    )(*map(on_chip, (fields, *factors)))
    shares = exchange(back, BACK)
    return pl.pallas_call(
        unpack_kernel,
        out_shape=(
            shape(XR, ny, LANES, dtype=BF16),
            shape(XR, LANES),
            shape(XR, LANES),
            shape(YU, LANES),
            shape(YU, LANES),
        ),
        scratch_shapes=[pltpu.VMEM((BACK * LANES, LANES), F32), pltpu.VMEM((TILES * LANES, LANES), F32)],
    )(on_chip(shares))


def solution(mesh):
    return jax.shard_map(
        on_device,
        mesh=mesh,
        in_specs=(
            P(("traj", "slab"), None, None),
            P("traj", "slab", None),
            P(("traj", "slab"), None, None),
            P("traj", None),
            P("traj", None),
            P("traj", None),
            P("traj", None),
        ),
        out_specs=(
            P(("traj", "slab"), None, None),
            P(("traj", "slab"), None),
            P(("traj", "slab"), None),
            P(("traj", "slab"), None),
            P(("traj", "slab"), None),
        ),
        check_vma=False,
    )
```

```python
import functools
import math

import jax
import jax.numpy as jnp
from jax import lax
from jax.experimental import pallas as pl
from jax.experimental.pallas import tpu as pltpu
from jax.sharding import PartitionSpec as P

HEAD = 32
LANES = 128
XR = 2
YU = 3
TILES = XR * YU
SEND = 3 * TILES
BACK = TILES + 4
Z, Y, CORES = 8, 8, 2
FIRST = (5, 4)
F32 = jnp.float32
BF16 = jnp.bfloat16
ROOT = math.sqrt(HEAD)


def dot(a, b, dims=((1,), (0,))):
    return lax.dot_general(a, b, (dims, ((), ())), preferred_element_type=F32)


def owner(p):
    z = (Z + FIRST[0] - p // (Y * CORES)) % Z
    y = (Y + FIRST[1] - p % Y) % Y
    return (z * Y + y) * CORES + CORES - 1 - p // Y % CORES


def place(s):
    z = (Z + FIRST[0] - s // (Y * CORES)) % Z
    y = (Y + FIRST[1] - s // CORES % Y) % Y
    return (z * CORES + CORES - 1 - s % CORES) * Y + y


def entry_kernel(
    grad_ref, cached_ref, values_ref, query_x_ref, key_x_ref, query_y_ref, key_y_ref,
    out_ref, tiled_qx_ref, tiled_kx_ref, placed_kx_ref, tiled_qy_ref, tiled_ky_ref, natural_ref, placed_ref,
    rows_ref, send_ref, factor_ref,
):
    for part, ref in enumerate((grad_ref, cached_ref, values_ref)):
        rows_ref[part] = ref[...].reshape(TILES * LANES, LANES).astype(F32)
        for u in range(YU):
            for r in range(XR):
                if part == 1:
                    tile = rows_ref[part, pl.ds(u * XR * LANES + r, LANES, stride=XR), :]
                else:
                    tile = rows_ref[part, pl.ds(r * YU * LANES + u, LANES, stride=YU), :]
                send_ref[pl.ds(part * TILES + u * XR + r, LANES, stride=SEND), :] = tile.T
    out_ref[...] = send_ref[...].astype(BF16)

    head = place(lax.axis_index("slab")) // HEAD
    source = lax.broadcasted_iota(jnp.int32, (LANES, LANES), 0)
    lane = lax.broadcasted_iota(jnp.int32, (LANES, LANES), 1)
    spread = (source == head * HEAD + lane % HEAD).astype(BF16)
    placed = (owner(source) == lane).astype(BF16)
    natural_ref[...] = (source == owner(lane)).astype(BF16)
    placed_ref[...] = placed

    def tiled(at, ref, step):
        factor_ref[at, 0 : step * LANES, :] = dot(ref[...], spread)
        blocks = [factor_ref[at, pl.ds(r, LANES, stride=step), :] for r in range(step)]
        return [block.astype(BF16) for block in blocks]

    def put(blocks):
        return jnp.concatenate([dot(placed, block) for block in blocks], axis=0).astype(BF16)

    query_x = tiled(0, query_x_ref, XR)
    key_x = tiled(1, key_x_ref, XR)
    tiled_qx_ref[...] = put(query_x)
    placed_kx_ref[...] = put(key_x)
    tiled_kx_ref[...] = jnp.concatenate(key_x, axis=0)
    tiled_qy_ref[...] = jnp.concatenate(tiled(2, query_y_ref, YU), axis=0)
    tiled_ky_ref[...] = jnp.concatenate(tiled(3, key_y_ref, YU), axis=0)


def softmax(tiled_q, tiled_k, axis):
    first = lax.broadcasted_iota(jnp.int32, tiled_q.shape, 1) < HEAD
    scores = dot(jnp.where(first, tiled_q, 0), tiled_k, ((1,), (1,))) / ROOT
    power = jnp.exp(scores - jnp.max(scores, axis=axis, keepdims=True))
    return power / jnp.sum(power, axis=axis, keepdims=True)


def channel_kernel(
    field_ref, tiled_qx_ref, tiled_kx_ref, placed_kx_ref, tiled_qy_ref, tiled_ky_ref, natural_ref, placed_ref,
    out_ref, rows_ref, back_ref,
):
    rows_ref[...] = field_ref[...].astype(F32)

    def tile(q):
        return rows_ref[pl.ds(q, LANES, stride=SEND), :].astype(BF16)

    def field(part):
        return jnp.concatenate(
            [
                jnp.concatenate([tile(part * TILES + u * XR + r) for u in range(YU)], axis=1)
                for r in range(XR)
            ],
            axis=0,
        )

    grad = field(0)
    values = field(2)
    cached = jnp.concatenate([tile(TILES + q) for q in range(TILES)], axis=1)
    cached = dot(natural_ref[...], cached).astype(BF16)
    cached = jnp.concatenate(
        [cached[:, u * XR * LANES : (u + 1) * XR * LANES] for u in range(YU)], axis=0
    )
    kernel_x = softmax(tiled_qx_ref[...], tiled_kx_ref[...], 1)
    kernel_xt = softmax(placed_kx_ref[...], tiled_qx_ref[...], 0)
    kernel_y = softmax(tiled_qy_ref[...], tiled_ky_ref[...], 1)
    mixed = dot(kernel_xt.astype(BF16), grad).astype(BF16)
    grad_values = dot(mixed, kernel_y.astype(BF16))
    for u in range(YU):
        for r in range(XR):
            back_ref[pl.ds(u * XR + r, LANES, stride=BACK), :] = grad_values[
                r * LANES : (r + 1) * LANES, u * LANES : (u + 1) * LANES
            ]

    def factor_grads(kernel, coupling, tiled_q, tiled_k):
        delta = jnp.sum(kernel * coupling, axis=1, keepdims=True)
        weighted = kernel * (coupling - delta) / ROOT
        high = weighted.astype(BF16)
        low = (weighted - high.astype(F32)).astype(BF16)
        grad_query = dot(high, tiled_k) + dot(low, tiled_k)
        turned_q = tiled_q.T
        grad_key = (dot(turned_q, high) + dot(turned_q, low)).T
        return grad_query, grad_key

    query_x, key_x = factor_grads(
        kernel_x, dot(grad, cached), tiled_qx_ref[...], tiled_kx_ref[...]
    )
    query_y, key_y = factor_grads(
        kernel_y, dot(mixed, values, ((0,), (0,))), tiled_qy_ref[...], tiled_ky_ref[...]
    )
    group = lax.broadcasted_iota(jnp.int32, (LANES, LANES), 1) // HEAD

    def line_up(slots):
        total = jnp.zeros((LANES, LANES), F32)
        for at, slot in slots:
            total = jnp.where(group == at, slot, total)
        return total

    slots = [key_x[r * LANES : (r + 1) * LANES] for r in range(XR)]
    slots += [query_y[u * LANES : (u + 1) * LANES] for u in range(YU)]
    slots += [key_y[u * LANES : (u + 1) * LANES] for u in range(YU)]
    lines = [line_up(zip((2, 3), slots[:2])), line_up(zip(range(4), slots[2:6])), line_up(zip((0, 1), slots[6:]))]
    lines = dot(placed_ref[...], jnp.concatenate(lines, axis=1).astype(BF16))
    first = line_up((r, query_x[r * LANES : (r + 1) * LANES]) for r in range(XR))
    back_ref[pl.ds(TILES, LANES, stride=BACK), :] = first + lines[:, :LANES]
    back_ref[pl.ds(TILES + 1, LANES, stride=BACK), :] = lines[:, LANES : 2 * LANES]
    back_ref[pl.ds(TILES + 2, LANES, stride=BACK), :] = lines[:, 2 * LANES :]
    back_ref[pl.ds(TILES + 3, LANES, stride=BACK), :] = jnp.zeros((LANES, LANES), F32)
    out_ref[...] = back_ref[...].astype(BF16)


def unpack_kernel(
    back_ref, values_ref, query_x_ref, key_x_ref, query_y_ref, key_y_ref, rows_ref, frame_ref
):
    rows_ref[...] = back_ref[...].astype(F32)
    for u in range(YU):
        for r in range(XR):
            tile = rows_ref[pl.ds(u * XR + r, LANES, stride=BACK), :]
            frame_ref[pl.ds(r * YU * LANES + u, LANES, stride=YU), :] = tile.T
    values_ref[...] = frame_ref[...].astype(BF16).reshape(values_ref.shape)
    source = lax.broadcasted_iota(jnp.int32, (LANES, 4 * LANES), 0)
    lane = lax.broadcasted_iota(jnp.int32, (LANES, 4 * LANES), 1)
    spread = (source == (lane // LANES) * HEAD + lane % HEAD).astype(BF16)
    own = source // HEAD == (lane % LANES) // HEAD
    sums = []
    for line in range(3):
        shares = rows_ref[pl.ds(TILES + line, LANES, stride=BACK), :].astype(BF16)
        total = jnp.sum(jnp.where(own, dot(shares, spread), 0.0), axis=0, keepdims=True)
        sums += [total[:, k * LANES : (k + 1) * LANES] for k in range(4)]
    for r in range(XR):
        query_x_ref[r : r + 1, :] = sums[r]
        key_x_ref[r : r + 1, :] = sums[XR + r]
    for u in range(YU):
        query_y_ref[u : u + 1, :] = sums[2 * XR + u]
        key_y_ref[u : u + 1, :] = sums[2 * XR + YU + u]


def shape(*dims, dtype=F32):
    return jax.ShapeDtypeStruct(dims, dtype)


def on_chip(array):
    return pltpu.with_memory_space_constraint(array, pltpu.VMEM)


def exchange(rows, count):
    parts = rows.reshape(LANES, count // 2, 2, LANES)
    order = [[owner(p) for p in range(LANES)]]
    moved = lax.all_to_all(
        parts, "slab", split_axis=0, concat_axis=0, tiled=True, axis_index_groups=order
    )
    return moved.reshape(LANES * count, LANES)


def on_device(grad_out, cached, values, query_x, key_x, query_y, key_y):
    nx, ny = XR * LANES, YU * LANES
    packed, *factors = pl.pallas_call(
        entry_kernel,
        out_shape=(
            pltpu.VMEM((SEND * LANES, LANES), BF16),
            pltpu.VMEM((nx, LANES), BF16),
            pltpu.VMEM((nx, LANES), BF16),
            pltpu.VMEM((nx, LANES), BF16),
            pltpu.VMEM((ny, LANES), BF16),
            pltpu.VMEM((ny, LANES), BF16),
            pltpu.VMEM((LANES, LANES), BF16),
            pltpu.VMEM((LANES, LANES), BF16),
        ),
        scratch_shapes=[
            pltpu.VMEM((3, TILES * LANES, LANES), F32),
            pltpu.VMEM((SEND * LANES, LANES), F32),
            pltpu.VMEM((4, ny, LANES), F32),
        ],
    )(grad_out, cached.transpose(1, 0, 2), values, query_x, key_x, query_y, key_y)
    fields = exchange(packed, SEND)
    back = pl.pallas_call(
        channel_kernel,
        out_shape=pltpu.VMEM((BACK * LANES, LANES), BF16),
        scratch_shapes=[pltpu.VMEM((SEND * LANES, LANES), F32), pltpu.VMEM((BACK * LANES, LANES), F32)],
    )(*map(on_chip, (fields, *factors)))
    shares = exchange(back, BACK)
    return pl.pallas_call(
        unpack_kernel,
        out_shape=(
            shape(XR, ny, LANES, dtype=BF16),
            shape(XR, LANES),
            shape(XR, LANES),
            shape(YU, LANES),
            shape(YU, LANES),
        ),
        scratch_shapes=[pltpu.VMEM((BACK * LANES, LANES), F32), pltpu.VMEM((TILES * LANES, LANES), F32)],
    )(on_chip(shares))


def solution(mesh):
    return jax.shard_map(
        on_device,
        mesh=mesh,
        in_specs=(
            P(("traj", "slab"), None, None),
            P("traj", "slab", None),
            P(("traj", "slab"), None, None),
            P("traj", None),
            P("traj", None),
            P("traj", None),
            P("traj", None),
        ),
        out_specs=(
            P(("traj", "slab"), None, None),
            P(("traj", "slab"), None),
            P(("traj", "slab"), None),
            P(("traj", "slab"), None),
            P(("traj", "slab"), None),
        ),
        check_vma=False,
    )
```
